256 devices in a mesh: blk: 32 (over y, x, z_hi), rows: 8 (over z_lo, core).
Axes of the slice: x: 4, y: 4, z: 8 (z_hi: 2, z_lo: 4; z = z_hi * 4 + z_lo), core: 2. Of those that a mesh axis runs over, the one named last changes fastest.
Arguments:
- target_pos: float32 [3, 65536], P(None, ('blk', 'rows')), may hold values from 0 to 5.03852
- target_len: float32 [65536], P(('blk', 'rows')), may hold values from 0.2 to 0.6
- cotangent: float32 [65536, 128], P(('blk', 'rows')), may hold values from -0.3125 to 0.3125
- source_pos: float32 [3, 32768], P(None, ('blk', 'rows')), may hold values from 0 to 5.03852
- source_len: float32 [32768], P(('blk', 'rows')), may hold values from 0.2 to 0.6
- vectors: float32 [32768, 128], P(('blk', 'rows')), may hold values from -6 to 6
Outputs:
- grad_vectors: float32 [32768, 128], P(('blk', 'rows'))
- grad_source_len: float32 [32768], P(('blk', 'rows'))
- grad_target_len: float32 [65536], P(('blk', 'rows'))
The draws below stay inside these ranges and needn't reach their ends.
All inputs are finite; a program needn't handle non-finite values.
Results may differ from the reference program's by a relative error of at most 0.0003.
Values sent between devices are 32-bit elements; how exact they have to be, the bound alone decides.
No kernel may reach another device: no remote copies, remote signals or barrier semaphores. Data moves between devices by JAX's collectives and lax.ppermute only.
A program may use at most 64 MiB of HBM per device.

```python
import math
import jax
import jax.numpy as jnp
from jax import lax

T_DEV = 256
S_DEV = 128
NVEC = 128
STEPS = 8
NT = 65536
NS = 32768
N_BLK = 32
N_ROWS = 8


def block_scale(key, extent, shards, low, high):
    gain, own = 1.0, jax.random.fold_in(key, 6)
    for axis_at, blocks in shards:
        heights = jnp.exp(jax.random.uniform(jax.random.fold_in(own, axis_at), (blocks,), jnp.float32, low / len(shards), high / len(shards)))
        gain = gain * jnp.repeat(heights, extent[axis_at] // blocks).reshape([-1 if axis == axis_at else 1 for axis in range(len(extent))])
    return gain


def noise(own_key, dims, spread, limit, shards=(), kind=jnp.bfloat16):
    values = spread * jax.random.normal(own_key, dims, jnp.float32)
    if shards:
        values = values * block_scale(own_key, dims, shards, -0.22, 0.18)
    return jnp.clip(values, -limit, limit).astype(kind)


def setup_inputs(seed: int = 0) -> dict:
    seeds = jax.random.split(jax.random.key(seed), 7)
    target_pos = jnp.clip(5.03852 * jax.random.uniform(seeds[0], (3, NT), jnp.float32) ** block_scale(seeds[0], (3, NT), ((1, 256),), -0.2, 0.2), 0.0, 5.03852)
    target_len = jnp.clip(jnp.exp(math.log(0.6) - 1.0986123 * jax.random.uniform(seeds[1], (NT,), jnp.float32) ** block_scale(seeds[1], (NT,), ((0, 256),), -0.2, 0.2)), 0.2, 0.6)
    cotangent = noise(seeds[2], (NT, NVEC), 0.05, 0.3125, ((0, 256),), jnp.float32)
    source_pos = jnp.clip(5.03852 * jax.random.uniform(seeds[3], (3, NS), jnp.float32) ** block_scale(seeds[3], (3, NS), ((1, 256),), -0.2, 0.2), 0.0, 5.03852)
    source_len = jnp.clip(jnp.exp(math.log(0.6) - 1.0986123 * jax.random.uniform(seeds[4], (NS,), jnp.float32) ** block_scale(seeds[4], (NS,), ((0, 256),), -0.2, 0.2)), 0.2, 0.6)
    vectors = noise(seeds[5], (NS, NVEC), 1.0, 6.0, ((0, 256),), jnp.float32)
    return {"target_pos": target_pos, "target_len": target_len, "cotangent": cotangent, "source_pos": source_pos, "source_len": source_len, "vectors": vectors}


def pair_terms(target_pos, target_len, cotangent, source_pos, source_len, vectors):
    dist_sq = jnp.zeros((target_len.shape[0], source_len.shape[0]), jnp.float32)
    for component in range(3):
        offset = target_pos[component][:, None] - source_pos[component][None, :]
        dist_sq = dist_sq + offset * offset
    scale_sum = target_len[:, None] * target_len[:, None] + source_len[None, :] * source_len[None, :]
    length_ratio = 2.0 * target_len[:, None] * source_len[None, :] / scale_sum
    kernel = length_ratio * jnp.sqrt(length_ratio) * jnp.exp(-dist_sq / scale_sum)
    products = jnp.dot(cotangent, vectors.T, precision=lax.Precision.HIGHEST)
    weighted = products * kernel
    shaped = weighted / scale_sum * (2.0 * dist_sq / scale_sum - 3.0)
    grad_target = target_len * lax.optimization_barrier(jnp.sum(shaped, 1)) + 1.5 / target_len * lax.optimization_barrier(jnp.sum(weighted, 1))
    grad_source = source_len * lax.optimization_barrier(jnp.sum(shaped, 0)) + 1.5 / source_len * lax.optimization_barrier(jnp.sum(weighted, 0))
    grad_vec = jnp.dot(kernel.T, cotangent, precision=lax.Precision.HIGHEST)
    return (grad_target, grad_vec, grad_source)

def reference(target_pos, target_len, cotangent, source_pos, source_len, vectors):
    group_size = T_DEV * N_ROWS
    block_size = S_DEV * N_ROWS

    def per_group(totals, group_index):
        grad_vectors, grad_source_len = totals
        target_start = (group_index * group_size).astype(jnp.int32)
        group_pos = lax.dynamic_slice_in_dim(target_pos, target_start, group_size, 1)
        group_len = lax.dynamic_slice_in_dim(target_len, target_start, group_size, 0)
        group_cot = lax.dynamic_slice_in_dim(cotangent, target_start, group_size, 0)
        grad_group = jnp.zeros((group_size,), jnp.float32)
        for cycle_step in range(STEPS):
            anchor = ((group_index - cycle_step) % N_BLK * block_size).astype(jnp.int32)
            block_pos = lax.dynamic_slice_in_dim(source_pos, anchor, block_size, 1)
            block_len = lax.dynamic_slice_in_dim(source_len, anchor, block_size, 0)
            block_vec = lax.dynamic_slice_in_dim(vectors, anchor, block_size, 0)
            grad_target, grad_vec, grad_source = pair_terms(group_pos, group_len, group_cot, block_pos, block_len, block_vec)
            grad_group = grad_group + grad_target
            old_vec = lax.dynamic_slice_in_dim(grad_vectors, anchor, block_size, 0)
            grad_vectors = lax.dynamic_update_slice_in_dim(grad_vectors, old_vec + grad_vec, anchor, 0)
            old_len = lax.dynamic_slice_in_dim(grad_source_len, anchor, block_size, 0)
            grad_source_len = lax.dynamic_update_slice_in_dim(grad_source_len, old_len + grad_source, anchor, 0)
        return ((grad_vectors, grad_source_len), grad_group)
    start_totals = (jnp.zeros((N_BLK * block_size, NVEC), jnp.float32), jnp.zeros((N_BLK * block_size,), jnp.float32))
    (grad_vectors, grad_source_len), groups = lax.scan(per_group, start_totals, jnp.arange(N_BLK, dtype=jnp.int32))
    return (grad_vectors, grad_source_len, groups.reshape(-1))
```

```python
import functools

import jax
import jax.numpy as jnp
from jax import lax
from jax.experimental import pallas as pl
from jax.experimental.pallas import tpu as pltpu
from jax.sharding import PartitionSpec as P
F32, BF16 = jnp.float32, jnp.bfloat16
LOG2E = 1.4426950408889634

def split(x):
    hi = x.astype(BF16)
    return hi, (x - hi.astype(F32)).astype(BF16)

def prep_body(*refs):
    parts, (c3, tm) = refs[:-2], refs[-2:]
    for n, part in enumerate(parts):
        hi, lo = split(part[0:256, :])
        c3[pl.ds(n*256, 256), :] = jnp.concatenate([hi, lo, hi], 1)
        for row in range(4):
            for half in range(2):
                tm[row:row+1, pl.ds(n*256 + half*128, 128)] = part[pl.ds(256 + 2*row + half, 1), :]

def prep(parts):
    n = len(parts)
    return pl.pallas_call(prep_body, out_shape=(jax.ShapeDtypeStruct((n*256, 384), BF16), jax.ShapeDtypeStruct((8, n*256), F32)), name="prep")(*parts)

CH=256
def pair_body(nk, jt, c3, tm, *refs):
    blocks = refs[:nk]
    outs = refs[nk:2*nk]
    tsum = refs[2*nk]
    v3s, cols, gacc, sacc = refs[2*nk+1:]
    step = pl.program_id(0)
    @pl.when(step == 0)
    def _():
        for k in range(nk):
            hi, lo = split(blocks[k][0:128, :])
            v3s[pl.ds(k*128, 128), :] = jnp.concatenate([hi, hi, lo], 1)
            cols[pl.ds(k*128, 128), :] = jnp.concatenate([jnp.transpose(blocks[k][128:136, :]),jnp.zeros((128,120),F32)],1)
        gacc[...] = jnp.zeros_like(gacc)
        sacc[...] = jnp.zeros_like(sacc)
    w = c3[...]
    chl = w[:, :256]
    tx, ty, tz, tl = (tm[r:r+1, :] for r in range(4))
    th = jnp.zeros((8, CH), F32); tw = jnp.zeros((8, CH), F32)
    for j in range(nk*128//jt):
        rows = pl.ds(j*jt, jt)
        prod = lax.dot_general(v3s[rows, :], w, (((1,), (1,)), ((), ())), preferred_element_type=F32)
        col = cols[rows, :]
        sx, sy, sz, sl = (col[:, r:r+1] for r in range(4))
        dx = tx - sx; dy = ty - sy; dz = tz - sz
        dist = dx*dx + dy*dy + dz*dz
        root = lax.rsqrt(tl + sl)
        inv = root*root
        q = dist*inv
        kern = (inv*root)*jnp.exp2(-q)
        weighted = prod*kern
        shaped = weighted*(inv*((2.0/LOG2E)*q - 3.0))
        hi, lo = split(kern)
        gacc[rows, :] += jnp.dot(hi, chl, preferred_element_type=F32) + jnp.dot(lo, chl, preferred_element_type=F32)
        sacc[rows, :] += sum(shaped[:, l*128:(l+1)*128] for l in range(CH//128))
        th = th + jnp.sum(shaped.reshape(jt//8, 8, CH), 0)
        tw = tw + jnp.sum(weighted.reshape(jt//8, 8, CH), 0)
    tsum[...] = jnp.concatenate([jnp.sum(th, 0, keepdims=True), jnp.sum(tw, 0, keepdims=True), jnp.zeros((6, CH), F32)], 0)
    @pl.when(step == pl.num_programs(0) - 1)
    def _():
        for k in range(nk):
            g = gacc[pl.ds(k*128, 128), :]
            outs[k][0:128, :] = g[:, :128] + g[:, 128:]
            s = jnp.sum(jnp.transpose(sacc[pl.ds(k*128, 128), :]), 0, keepdims=True)
            outs[k][128:136, :] = jnp.concatenate([s, jnp.zeros((7, 128), F32)], 0)

def pair(c3, tm, blocks, jt=128):
    nk = len(blocks); nt = c3.shape[0]
    full = pl.BlockSpec((136, 128), lambda i: (0, 0))
    return pl.pallas_call(
        functools.partial(pair_body, nk, jt),
        grid=(nt//CH,),
        in_specs=[pl.BlockSpec((CH, 384), lambda i: (i, 0)), pl.BlockSpec((8, CH), lambda i: (0, i))] + [full]*nk,
        out_specs=[full]*nk + [pl.BlockSpec((8, CH), lambda i: (0, i))],
        out_shape=[jax.ShapeDtypeStruct((136, 128), F32)]*nk + [jax.ShapeDtypeStruct((8, nt), F32)],
        scratch_shapes=[pltpu.VMEM((nk*128, 384), BF16), pltpu.VMEM((nk*128, 128), F32), pltpu.VMEM((nk*128, 256), F32), pltpu.VMEM((nk*128, 128), F32)],
        name="pair%d" % nk,
    )(c3, tm, *blocks)


def send(block, axis, target):
    return lax.ppermute(block, axis, [(i, target(i)) for i in range(lax.axis_size(axis))])


def flip(block):
    return send(block, "blk", lambda i: i ^ 1)


def ahead(block, distance):
    n = lax.axis_size("blk")
    return send(block, "blk", lambda i: (i + 2 * distance) % n)


def across(block, sign):
    n = lax.axis_size("blk")
    return send(block, "blk", lambda i: i if i % 2 else (i + 8 * sign) % n)


def row_send(block, mask):
    return send(block, "rows", lambda i: i ^ mask)


def shards(target_pos, target_len, cotangent, source_pos, source_len, vectors):
    scale = LOG2E ** 0.5
    target_gain = (2.0 * target_len) * jnp.sqrt(2.0 * target_len)
    source_gain = source_len * jnp.sqrt(source_len)
    target = jnp.concatenate([
        cotangent * target_gain[:, None],
        (target_pos * scale).reshape(6, 128),
        (target_len * target_len).reshape(2, 128)], 0)
    source = jnp.concatenate([
        vectors * source_gain[:, None], source_pos * scale,
        (source_len * source_len)[None], jnp.zeros((4, 128), F32)], 0)

    other = flip(source)
    z_parts = [target] + [row_send(target, 2 * k) for k in (1, 2, 3)]
    core_parts = [row_send(part, 1) for part in z_parts]
    parts = [part for pair_of in zip(z_parts, core_parts) for part in pair_of]
    near = [None] + [ahead(source, d) for d in (1, 2, 3)]
    far = [across(other, 1)] + [ahead(other, d) for d in (1, 2, 3)]

    c3, tm = prep(parts)
    far_out = pair(c3, tm, [far[3], far[2], far[1], far[0]])
    far_sum = ahead(far_out[0], -3) + ahead(far_out[1], -2) + ahead(far_out[2], -1) + across(far_out[3], -1)
    near_out = pair(c3, tm, [near[3], near[2], near[1], source])
    total = near_out[3] + flip(far_sum)
    for n, d in enumerate((3, 2, 1)):
        total = total + ahead(near_out[n], -d)

    sums = (far_out[4] + near_out[4])[:2].reshape(2, 8, 256).transpose(1, 0, 2).reshape(4, 2, 4, 128)
    chip = sums[:, 0] + row_send(sums[:, 1], 1)
    target_sums = (chip[0] + row_send(chip[1], 2) + row_send(chip[2], 4) + row_send(chip[3], 6)).reshape(2, 256)
    grad_target_len = target_len * target_sums[0] + 1.5 / target_len * target_sums[1]

    grad_vectors = total[:128] * source_gain[:, None]
    grad_source_len = source_len * total[128] + 1.5 / source_len * jnp.sum(vectors * grad_vectors, 1)
    return (grad_vectors, grad_source_len, grad_target_len)


def solution(mesh):
    placed = (
        P(None, ("blk", "rows")),
        P(("blk", "rows")),
        P(("blk", "rows"), None),
        P(None, ("blk", "rows")),
        P(("blk", "rows")),
        P(("blk", "rows"), None),
    )
    return jax.shard_map(
        shards,
        mesh=mesh,
        in_specs=placed,
        out_specs=(P(("blk", "rows"), None), P(("blk", "rows")), P(("blk", "rows"))),
        check_vma=False,
    )
```

```python
import functools

import jax
import jax.numpy as jnp
from jax import lax
from jax.experimental import pallas as pl
from jax.experimental.pallas import tpu as pltpu
from jax.sharding import PartitionSpec as P


F32, BF16 = jnp.float32, jnp.bfloat16
LOG2E = 1.4426950408889634
SCALE = LOG2E ** 0.5
MID = 2.51926
T_ROWS, S_ROWS, LANES = 264, 136, 128
TILE = 64


def split(x):
    hi = x.astype(BF16)
    return hi, (x - hi.astype(F32)).astype(BF16)


def split3(x):
    a = x.astype(BF16).astype(F32)
    b = (x - a).astype(BF16).astype(F32)
    return a, b, (x - a - b).astype(BF16).astype(F32)


def norm_of(x, y, z):
    return x * x + y * y + z * z


def target_rows(x, y, z):
    rows = []
    for value in (x, y, z):
        a, b, c = split3(value)
        rows += [a, b, a, c, a, b]
    rows += list(split3(norm_of(x, y, z))) + [jnp.ones_like(x)] * 3 + [jnp.zeros_like(x)] * 8
    return jnp.concatenate(rows, 0)


def source_rows(x, y, z):
    rows = []
    for value in (x, y, z):
        a, b, c = split3(value)
        rows += [2 * a, 2 * a, 2 * b, 2 * a, 2 * c, 2 * b]
    rows += [-jnp.ones_like(x)] * 3 + [-r for r in split3(norm_of(x, y, z))] + [jnp.zeros_like(x)] * 8
    return jnp.concatenate(rows, 0)


def column(row):
    return jnp.transpose(jnp.broadcast_to(row, (LANES, LANES)))


def call(body, inputs, outs, scratch=(), held=None, flops=0):
    vmem = pl.BlockSpec(memory_space=pltpu.VMEM)
    held = len(inputs) if held is None else held
    return pl.pallas_call(
        body,
        out_shape=outs,
        in_specs=[vmem] * len(inputs),
        scratch_shapes=scratch,
        cost_estimate=pl.CostEstimate(flops=flops, transcendentals=0, bytes_accessed=0),
    )(*[pltpu.with_memory_space_constraint(x, pltpu.VMEM) for x in inputs[:held]], *inputs[held:])


def pack_body(t_pos, t_len, cot, s_pos, s_len, vec, target, source):
    length = s_len[...].reshape(1, LANES)
    source[0:LANES, :] = vec[...] * column(length * jnp.sqrt(length))
    source[LANES:S_ROWS, :] = jnp.concatenate(
        [(s_pos[...] - MID) * SCALE, length * length, jnp.zeros((4, LANES), F32)], 0)
    pos = (t_pos[...] - MID) * SCALE
    meta = []
    for half in range(2):
        lanes = slice(half * LANES, (half + 1) * LANES)
        length = 2.0 * t_len[lanes].reshape(1, LANES)
        target[lanes, :] = cot[lanes, :] * column(length * jnp.sqrt(length))
        meta += [pos[:, lanes], 0.25 * length * length]
    target[2 * LANES:T_ROWS, :] = jnp.concatenate(meta, 0)


def pair_body(count, parts_n, *refs):
    parts, refs = refs[:parts_n], refs[parts_n:]
    blocks, refs = refs[:count], refs[count:]
    outs, refs = refs[:count], refs[count:]
    sums, vec3, feats, lens2, grads, rowsum, cots, prods, dists, highs, lows = refs
    blocks = [b.at[pl.ds(o, S_ROWS), :] for b in blocks for o in range(0, b.shape[0], S_ROWS)]
    outs = [b.at[pl.ds(o, S_ROWS), :] for b in outs for o in range(0, b.shape[0], S_ROWS)]
    total = len(blocks) * LANES
    width = 2 * LANES
    for k, block in enumerate(blocks):
        rows = pl.ds(k * LANES, LANES)
        hi, lo = split(block[0:LANES, :])
        vec3[rows, :] = jnp.concatenate([hi, hi, lo], 1)
        meta = block[LANES:S_ROWS, :]
        feats[rows, :] = jnp.transpose(source_rows(meta[0:1], meta[1:2], meta[2:3])).astype(BF16)
        lens2[rows, :] = column(meta[3:4])

    def first(c):
        hi, lo = split(parts[c][0:width, :])
        cots[c] = jnp.concatenate([hi, lo, hi], 1)
        meta = parts[c][width:T_ROWS, :]
        rows = [target_rows(*(meta[4 * h + r:4 * h + r + 1] for r in range(3))) for h in range(2)]
        prods[c % 2] = lax.dot_general(
            vec3[...], cots[c], (((1,), (1,)), ((), ())), preferred_element_type=F32)
        dists[c % 2] = jnp.dot(
            feats[...], jnp.concatenate(rows, 1).astype(BF16), preferred_element_type=F32)

    def middle(c):
        t_shaped = jnp.zeros((8, width), F32)
        t_weighted = jnp.zeros((8, width), F32)
        meta = parts[c][width:T_ROWS, :]
        t_len2 = jnp.concatenate([meta[3:4], meta[7:8]], 1)
        t_len2 = jnp.broadcast_to(t_len2, (TILE, width))
        for j in range(total // TILE):
            rows = pl.ds(j * TILE, TILE)
            s_len2 = lens2[rows, :]
            root = lax.rsqrt(t_len2 + jnp.concatenate([s_len2, s_len2], 1))
            inverse = root * root
            exponent = dists[c % 2, rows, :] * inverse
            kernel = (inverse * root) * jnp.exp2(exponent)
            weighted = prods[c % 2, rows, :] * kernel
            shaped = weighted * (inverse * (exponent + 1.5 * LOG2E))
            hi, lo = split(kernel)
            highs[c % 2, rows, :] = hi
            lows[c % 2, rows, :] = lo
            part = shaped[:, :LANES] + shaped[:, LANES:]
            rowsum[rows, :] = part if c == 0 else rowsum[rows, :] + part
            t_shaped += jnp.sum(shaped.reshape(TILE // 8, 8, width), 0)
            t_weighted += jnp.sum(weighted.reshape(TILE // 8, 8, width), 0)
        t_shaped = jnp.sum(t_shaped, 0, keepdims=True) * (-2.0 / LOG2E)
        t_weighted = jnp.sum(t_weighted, 0, keepdims=True)
        halves = [t_shaped[:, :LANES], t_shaped[:, LANES:], t_weighted[:, :LANES], t_weighted[:, LANES:]]
        sums[c // 2 + parts_n // 2 * (c % 2)] = jnp.concatenate(halves + [jnp.zeros((4, LANES), F32)], 0)

    def last(c):
        cot = cots[c, :, 0:width]
        part = jnp.dot(highs[c % 2], cot, preferred_element_type=F32)
        part += jnp.dot(lows[c % 2], cot, preferred_element_type=F32)
        grads[...] = part if c == 0 else grads[...] + part

    first(0)
    for c in range(parts_n):
        if c + 1 < parts_n:
            first(c + 1)
        middle(c)
        if c:
            last(c - 1)
    last(parts_n - 1)
    for k, out in enumerate(outs):
        rows = pl.ds(k * LANES, LANES)
        out[0:LANES, :] = grads[rows, :LANES] + grads[rows, LANES:]
        row = jnp.sum(jnp.transpose(rowsum[rows, :]), 0, keepdims=True) * (-2.0 / LOG2E)
        out[LANES:S_ROWS, :] = jnp.concatenate([row, jnp.zeros((7, LANES), F32)], 0)


def pair(parts, blocks):
    n = len(parts)
    total = sum(b.shape[0] for b in blocks) // S_ROWS * LANES
    width = 2 * LANES
    return call(
        functools.partial(pair_body, len(blocks), n), list(parts) + list(blocks),
        [pltpu.VMEM(b.shape, F32) for b in blocks] + [pltpu.VMEM((n, 8, LANES), F32)],
        [
            pltpu.VMEM((total, 3 * LANES), BF16), pltpu.VMEM((total, 32), BF16),
            pltpu.VMEM((total, LANES), F32), pltpu.VMEM((total, width), F32),
            pltpu.VMEM((total, LANES), F32), pltpu.VMEM((n, width, 3 * LANES), BF16),
            pltpu.VMEM((2, total, width), F32), pltpu.VMEM((2, total, width), F32),
            pltpu.VMEM((2, total, width), BF16), pltpu.VMEM((2, total, width), BF16),
        ],
        flops=8 * 10 ** 9,
    )


def finish_body(own, near1, near2, near3, far, own_sums, near_sums, s_len, vec, t_len,
                grad_vec, grad_s, grad_t):
    total = own[...] + far[...] + near1[...] + near2[...] + near3[...]
    length = s_len[...].reshape(1, LANES)
    grad = total[0:LANES, :] * column(length * jnp.sqrt(length))
    grad_vec[...] = grad
    weighted = jnp.sum(jnp.transpose(vec[...] * grad), 0, keepdims=True)
    grad_s[...] = (length * total[LANES:LANES + 1, :] + 1.5 / length * weighted).reshape(LANES)
    sums = own_sums[...] + near_sums[...]
    for half in range(2):
        lanes = slice(half * LANES, (half + 1) * LANES)
        length = t_len[lanes].reshape(1, LANES)
        grad_t[lanes] = (length * sums[half:half + 1] + 1.5 / length * sums[2 + half:3 + half]).reshape(LANES)


def send(block, axis, target):
    return lax.ppermute(block, axis, [(i, target(i)) for i in range(lax.axis_size(axis))])


def flip(block):
    return send(block, "blk", lambda i: i ^ 1)


def ahead(block, distance):
    n = lax.axis_size("blk")
    return send(block, "blk", lambda i: (i + 2 * distance) % n)


def across(block, sign):
    n = lax.axis_size("blk")
    return send(block, "blk", lambda i: i if i % 2 else (i + 8 * sign) % n)


def row_send(block, mask):
    return send(block, "rows", lambda i: i ^ mask)


def device_part(target_pos, target_len, cotangent, source_pos, source_len, vectors):
    target, source = call(
        pack_body, [target_pos, target_len, cotangent, source_pos, source_len, vectors],
        [pltpu.VMEM((T_ROWS, LANES), F32), pltpu.VMEM((S_ROWS, LANES), F32)], held=0)
    other = flip(source)
    z_parts = [target] + [row_send(target, 2 * k) for k in (1, 2, 3)]
    core_parts = [row_send(part, 1) for part in z_parts]
    parts = [part for pair_of in zip(z_parts, core_parts) for part in pair_of]
    near = [ahead(source, d) for d in (1, 2, 3)]
    far = [ahead(other, d) for d in (1, 2, 3)]

    *far_grads, g_across, sums_far = pair(parts, far + [across(other, 1)])
    far_sum = across(g_across, -1)
    for d in (3, 2, 1):
        far_sum = far_sum + ahead(far_grads[d - 1], -d)
    *near_grads, g_own, sums_near = pair(parts, near + [source])
    far_sum = flip(far_sum)
    near_grads = [ahead(near_grads[d - 1], -d) for d in (1, 2, 3)]

    sums = sums_far + sums_near
    chip = sums[0:4] + row_send(sums[4:8], 1)
    half = chip[0:2] + row_send(chip[2:4], 4)
    last = row_send(half[1], 2)

    outs = [
        jax.ShapeDtypeStruct((LANES, LANES), F32),
        jax.ShapeDtypeStruct((LANES,), F32),
        jax.ShapeDtypeStruct((2 * LANES,), F32),
    ]
    inputs = [g_own, *near_grads, far_sum, half[0], last, source_len, vectors, target_len]
    return call(finish_body, inputs, outs, held=7)


def solution(mesh):
    placed = (
        P(None, ("blk", "rows")),
        P(("blk", "rows")),
        P(("blk", "rows"), None),
        P(None, ("blk", "rows")),
        P(("blk", "rows")),
        P(("blk", "rows"), None),
    )
    return jax.shard_map(
        device_part,
        mesh=mesh,
        in_specs=placed,
        out_specs=(P(("blk", "rows"), None), P(("blk", "rows")), P(("blk", "rows"))),
        check_vma=False,
    )
```

```python
import functools

import jax
import jax.numpy as jnp
from jax import lax
from jax.experimental import pallas as pl
from jax.experimental.pallas import tpu as pltpu
from jax.sharding import PartitionSpec as P


F32, BF16 = jnp.float32, jnp.bfloat16
LOG2E = 1.4426950408889634
SCALE = LOG2E ** 0.5
MID = 2.51926
T_ROWS, S_ROWS, LANES = 264, 136, 128
TILE = 64


def split(x):
    hi = x.astype(BF16)
    return hi, (x - hi.astype(F32)).astype(BF16)


def split3(x):
    a = x.astype(BF16).astype(F32)
    b = (x - a).astype(BF16).astype(F32)
    return a, b, (x - a - b).astype(BF16).astype(F32)


def norm_of(x, y, z):
    return x * x + y * y + z * z


def target_rows(x, y, z):
    rows = []
    for value in (x, y, z):
        a, b, c = split3(value)
        rows += [a, b, a, c, a, b]
    rows += list(split3(norm_of(x, y, z))) + [jnp.ones_like(x)] * 3 + [jnp.zeros_like(x)] * 8
    return jnp.concatenate(rows, 0)


def source_rows(x, y, z):
    rows = []
    for value in (x, y, z):
        a, b, c = split3(value)
        rows += [2 * a, 2 * a, 2 * b, 2 * a, 2 * c, 2 * b]
    rows += [-jnp.ones_like(x)] * 3 + [-r for r in split3(norm_of(x, y, z))] + [jnp.zeros_like(x)] * 8
    return jnp.concatenate(rows, 0)


def column(row):
    return jnp.transpose(jnp.broadcast_to(row, (LANES, LANES)))


def call(body, inputs, outs, scratch=(), held=None, flops=0):
    vmem = pl.BlockSpec(memory_space=pltpu.VMEM)
    held = len(inputs) if held is None else held
    return pl.pallas_call(
        body,
        out_shape=outs,
        in_specs=[vmem] * len(inputs),
        scratch_shapes=scratch,
        cost_estimate=pl.CostEstimate(flops=flops, transcendentals=0, bytes_accessed=0),
    )(*[pltpu.with_memory_space_constraint(x, pltpu.VMEM) for x in inputs[:held]], *inputs[held:])


def pack_body(t_pos, t_len, cot, s_pos, s_len, vec, target, source, kept, lens):
    length = s_len[...].reshape(1, LANES)
    kept[...] = vec[...]
    lens[0:1, :] = length
    source[0:LANES, :] = vec[...] * column(length * jnp.sqrt(length))
    source[LANES:S_ROWS, :] = jnp.concatenate(
        [(s_pos[...] - MID) * SCALE, length * length, jnp.zeros((4, LANES), F32)], 0)
    pos = (t_pos[...] - MID) * SCALE
    meta = []
    for half in range(2):
        lanes = slice(half * LANES, (half + 1) * LANES)
        lens[1 + half:2 + half, :] = t_len[lanes].reshape(1, LANES)
        length = 2.0 * lens[1 + half:2 + half, :]
        target[lanes, :] = cot[lanes, :] * column(length * jnp.sqrt(length))
        meta += [pos[:, lanes], 0.25 * length * length]
    target[2 * LANES:T_ROWS, :] = jnp.concatenate(meta, 0)


def pair_body(count, parts_n, before, *refs):
    parts, refs = refs[:parts_n], refs[parts_n:]
    blocks, refs = refs[:count], refs[count:]
    if before:
        earlier, refs = refs[:count], refs[count:]
        far_sums, early_sums, refs = refs[0], refs[1], refs[2:]
    outs, refs = refs[:count], refs[count:]
    sums, vec3, feats, lens2, grads, rowsum, cots, prods, dists, highs, lows = refs
    total = count * LANES
    width = 2 * LANES
    for k, block in enumerate(blocks):
        rows = pl.ds(k * LANES, LANES)
        hi, lo = split(block[0:LANES, :])
        vec3[rows, :] = jnp.concatenate([hi, hi, lo], 1)
        meta = block[LANES:S_ROWS, :]
        feats[rows, :] = jnp.transpose(source_rows(meta[0:1], meta[1:2], meta[2:3])).astype(BF16)
        lens2[rows, :] = column(meta[3:4])

    def first(c):
        hi, lo = split(parts[c][0:width, :])
        cots[c] = jnp.concatenate([hi, lo, hi], 1)
        meta = parts[c][width:T_ROWS, :]
        rows = [target_rows(*(meta[4 * h + r:4 * h + r + 1] for r in range(3))) for h in range(2)]
        prods[c % 2] = lax.dot_general(
            vec3[...], cots[c], (((1,), (1,)), ((), ())), preferred_element_type=F32)
        dists[c % 2] = jnp.dot(
            feats[...], jnp.concatenate(rows, 1).astype(BF16), preferred_element_type=F32)

    def middle(c):
        t_shaped = jnp.zeros((8, width), F32)
        t_weighted = jnp.zeros((8, width), F32)
        meta = parts[c][width:T_ROWS, :]
        t_len2 = jnp.concatenate([meta[3:4], meta[7:8]], 1)
        t_len2 = jnp.broadcast_to(t_len2, (TILE, width))
        for j in range(total // TILE):
            rows = pl.ds(j * TILE, TILE)
            s_len2 = lens2[rows, :]
            root = lax.rsqrt(t_len2 + jnp.concatenate([s_len2, s_len2], 1))
            inverse = root * root
            exponent = dists[c % 2, rows, :] * inverse
            kernel = (inverse * root) * jnp.exp2(exponent)
            weighted = prods[c % 2, rows, :] * kernel
            shaped = weighted * (inverse * (exponent + 1.5 * LOG2E))
            hi, lo = split(kernel)
            highs[c % 2, rows, :] = hi
            lows[c % 2, rows, :] = lo
            part = shaped[:, :LANES] + shaped[:, LANES:]
            rowsum[rows, :] = part if c == 0 else rowsum[rows, :] + part
            t_shaped += jnp.sum(shaped.reshape(TILE // 8, 8, width), 0)
            t_weighted += jnp.sum(weighted.reshape(TILE // 8, 8, width), 0)
        t_shaped = jnp.sum(t_shaped, 0, keepdims=True) * (-2.0 / LOG2E)
        t_weighted = jnp.sum(t_weighted, 0, keepdims=True)
        halves = [t_shaped[:, :LANES], t_shaped[:, LANES:], t_weighted[:, :LANES], t_weighted[:, LANES:]]
        row = jnp.concatenate(halves + [jnp.zeros((4, LANES), F32)], 0)
        if before:
            row += far_sums[parts_n + c]
            sums[c % 2, (parts_n + c) // 2] = row
            sums[c % 2, c // 2] = far_sums[c] + early_sums[c]
        else:
            sums[c] = row

    def last(c):
        cot = cots[c, :, 0:width]
        part = jnp.dot(highs[c % 2], cot, preferred_element_type=F32)
        part += jnp.dot(lows[c % 2], cot, preferred_element_type=F32)
        grads[...] = part if c == 0 else grads[...] + part

    first(0)
    for c in range(parts_n):
        if c + 1 < parts_n:
            first(c + 1)
        middle(c)
        if c:
            last(c - 1)
    last(parts_n - 1)
    for k, out in enumerate(outs):
        rows = pl.ds(k * LANES, LANES)
        grad = grads[rows, :LANES] + grads[rows, LANES:]
        row = jnp.sum(jnp.transpose(rowsum[rows, :]), 0, keepdims=True) * (-2.0 / LOG2E)
        row = jnp.concatenate([row, jnp.zeros((7, LANES), F32)], 0)
        if before:
            grad += earlier[k][0:LANES, :]
            row += earlier[k][LANES:S_ROWS, :]
        out[0:LANES, :] = grad
        out[LANES:S_ROWS, :] = row


def pair(parts, blocks, before=()):
    n, count = len(parts), len(blocks)
    total = count * LANES
    width = 2 * LANES
    sums = (2, n, 8, LANES) if before else (n, 8, LANES)
    return call(
        functools.partial(pair_body, count, n, bool(before)), [*parts, *blocks, *before],
        [pltpu.VMEM((S_ROWS, LANES), F32)] * count + [pltpu.VMEM(sums, F32)],
        [
            pltpu.VMEM((total, 3 * LANES), BF16), pltpu.VMEM((total, 32), BF16),
            pltpu.VMEM((total, LANES), F32), pltpu.VMEM((total, width), F32),
            pltpu.VMEM((total, LANES), F32), pltpu.VMEM((n, width, 3 * LANES), BF16),
            pltpu.VMEM((2, total, width), F32), pltpu.VMEM((2, total, width), F32),
            pltpu.VMEM((2, total, width), BF16), pltpu.VMEM((2, total, width), BF16),
        ],
        flops=2 * n * count * 10 ** 8,
    )


def finish_body(own, near1, near2, near3, far, own_sums, near_sums, vec, lens,
                grad_vec, grad_s, grad_t):
    total = own[...] + far[...] + near1[...] + near2[...] + near3[...]
    length = lens[0:1, :]
    grad = total[0:LANES, :] * column(length * jnp.sqrt(length))
    grad_vec[...] = grad
    weighted = jnp.sum(jnp.transpose(vec[...] * grad), 0, keepdims=True)
    grad_s[...] = (length * total[LANES:LANES + 1, :] + 1.5 / length * weighted).reshape(LANES)
    sums = own_sums[...] + near_sums[...]
    for half in range(2):
        lanes = slice(half * LANES, (half + 1) * LANES)
        length = lens[1 + half:2 + half, :]
        grad_t[lanes] = (length * sums[half:half + 1] + 1.5 / length * sums[2 + half:3 + half]).reshape(LANES)


def send(block, axis, target):
    return lax.ppermute(block, axis, [(i, target(i)) for i in range(lax.axis_size(axis))])


def flip(block):
    return send(block, "blk", lambda i: i ^ 1)


def ahead(block, distance):
    n = lax.axis_size("blk")
    return send(block, "blk", lambda i: (i + 2 * distance) % n)


def across(block, sign):
    n = lax.axis_size("blk")
    return send(block, "blk", lambda i: i if i % 2 else (i + 8 * sign) % n)


def row_send(block, mask):
    return send(block, "rows", lambda i: i ^ mask)


def device_part(target_pos, target_len, cotangent, source_pos, source_len, vectors):
    target, source, kept, lens = call(
        pack_body, [target_pos, target_len, cotangent, source_pos, source_len, vectors],
        [pltpu.VMEM((rows, LANES), F32) for rows in (T_ROWS, S_ROWS, LANES, 8)], held=0)
    other = flip(source)
    z_parts = [target] + [row_send(target, 2 * k) for k in (1, 2, 3)]
    core_parts = [row_send(part, 1) for part in z_parts]
    parts = [part for pair_of in zip(z_parts, core_parts) for part in pair_of]
    near = [ahead(source, d) for d in (1, 2, 3)] + [source]
    far = [ahead(other, d) for d in (1, 2, 3)] + [across(other, 1)]

    *early_grads, early_sums = pair(parts[:4], near)
    *far_grads, far_sums = pair(parts, far)
    far_grads = [ahead(far_grads[d - 1], -d) for d in (1, 2, 3)] + [
        across(far_grads[3], -1)]
    *near_grads, g_own, sums = pair(parts[4:], near, [*early_grads, far_sums, early_sums])
    far_grad = flip(far_grads[0] + far_grads[1] + far_grads[2] + far_grads[3])
    near_grads = [ahead(near_grads[d - 1], -d) for d in (1, 2, 3)]

    chip = sums[0] + row_send(sums[1], 1)
    half = chip[0:2] + row_send(chip[2:4], 4)
    last = row_send(half[1], 2)

    outs = [
        jax.ShapeDtypeStruct((LANES, LANES), F32),
        jax.ShapeDtypeStruct((LANES,), F32),
        jax.ShapeDtypeStruct((2 * LANES,), F32),
    ]
    return call(finish_body, [g_own, *near_grads, far_grad, half[0], last, kept, lens], outs)


def solution(mesh):
    placed = (
        P(None, ("blk", "rows")),
        P(("blk", "rows")),
        P(("blk", "rows"), None),
        P(None, ("blk", "rows")),
        P(("blk", "rows")),
        P(("blk", "rows"), None),
    )
    return jax.shard_map(
        device_part,
        mesh=mesh,
        in_specs=placed,
        out_specs=(P(("blk", "rows"), None), P(("blk", "rows")), P(("blk", "rows"))),
        check_vma=False,
    )
```
